128 devices in a mesh: hid: 16 (over x, y), wid: 4 (over z_lo, core), rep: 2 (over z_hi).
Axes of the slice: x: 4, y: 4, z: 4 (z_hi: 2, z_lo: 2; z = z_hi * 2 + z_lo), core: 2. Of those that a mesh axis runs over, the one named last changes fastest.
Arguments:
- grad_out: bfloat16 [2, 1024, 8192], P('rep', None, 'wid'), may hold values from -6 to 6
- down_weight: bfloat16 [28672, 8192], P('hid', 'wid'), may hold values from -0.03125 to 0.03125
- saved_gate: bfloat16 [2, 1024, 28672], P('rep', 'wid', 'hid'), may hold values from -6 to 6
- saved_up: bfloat16 [2, 1024, 28672], P('rep', 'wid', 'hid'), may hold values from -6 to 6
- saved_codes: int32 [2, 1024, 28672], P('rep', 'wid', 'hid'), may hold values from -128 to 127, as said below
- exponents: int32 [2, 1024, 224], P('rep', 'wid', 'hid'), may hold values from -12 to -9
Outputs:
- grad_gate: bfloat16 [2, 1024, 28672], P('rep', 'wid', 'hid')
- grad_up: bfloat16 [2, 1024, 28672], P('rep', 'wid', 'hid')
- grad_down: float32 [28672, 8192], P('hid', ('wid', 'rep'))
The draws below stay inside these ranges and needn't reach their ends.
Inputs may be any that keep to these rules, and one draw needn't show every extreme that they name: `saved_codes`: codes at the clip limits -128 and 127 both occur.
All inputs are finite; a program needn't handle non-finite values.
Results may differ from the reference program's by a relative error of at most 0.014.
Values may be sent and summed in bfloat16 or wider, within the bound.
No kernel may reach another device: no remote copies, remote signals or barrier semaphores. Data moves between devices by JAX's collectives and lax.ppermute only.
A program may use at most 128 MiB of HBM per device.

```python
import math
import jax
import jax.numpy as jnp
from jax import lax

D = 8192
FF = 28672
BLOCK = 128
REPS = 2
GROUPS = 16
SLICES = 4
GROUP_TOK = 1024


def draw_saved_codes(key, part):
    raw_values = jax.random.randint(key, (REPS, GROUP_TOK, FF), -160, 160, dtype=jnp.int32)
    return jnp.clip(raw_values, -128, 127)


def touch_ends(array, key, least, largest):
    spot = [jax.random.randint(jax.random.fold_in(key, axis), (), 0, length) for axis, length in enumerate(array.shape)]
    longest = array.shape.index(max(array.shape))
    neighbour = spot[:longest] + [(spot[longest] + 1) % array.shape[longest]] + spot[longest + 1:]
    return array.at[tuple(spot)].set(least).at[tuple(neighbour)].set(largest)


def strengthened(values, key, source, target, parts, factor):
    owner, partner = [(jnp.arange(values.shape[dim]) // (values.shape[dim] // parts)).reshape([-1 if axis == dim else 1 for axis in range(values.ndim)]) for dim in (source, target)]
    chosen = jax.random.permutation(key, parts)[partner]
    strong = (owner == chosen) | (owner == (partner + parts // 2) % parts)
    return jnp.where(strong, factor * values, values)


def level_of(stream_key, extent, split, low, high):
    def one(position, shards_of):
        steps = jax.random.uniform(jax.random.fold_in(jax.random.fold_in(stream_key, 6), position), (shards_of,), jnp.float32, low / len(split), high / len(split))
        return jnp.repeat(jnp.exp(steps), extent[position] // shards_of).reshape((-1,) + (1,) * (len(extent) - position - 1))

    level = one(*split[0])
    for cut in split[1:]:
        level = level * one(*cut)
    return level


def gaussian(stream_key, extent, width, bound, shards=(), kind=jnp.bfloat16):
    factor_of = level_of(stream_key, extent, shards, -0.22, 0.18) if shards else 1.0
    result = jax.random.normal(stream_key, extent, jnp.float32) * width * factor_of
    return jnp.minimum(jnp.maximum(result, -bound), bound).astype(kind)


def bell_draw_with(rng, dims, spread, limit, shards, heavy, kind=jnp.bfloat16):
    result = spread * jax.random.normal(rng, dims, jnp.float32)
    if shards:
        result = result * level_of(rng, dims, shards, -0.22, 0.18)
    return jnp.clip(strengthened(result, jax.random.fold_in(rng, 3), *heavy), -limit, limit).astype(kind)


def setup_inputs(seed: int = 0) -> dict:
    seeds = jax.random.split(jax.random.key(seed), 7)
    grad_out = bell_draw_with(seeds[0], (REPS, GROUP_TOK, D), 1.0, 6.0, ((0, 2), (2, 4)), (2, 1, 4, 2.0))
    down_weight = gaussian(seeds[1], (FF, D), FF ** -0.5, 0.03125, ((0, 16), (1, 4)))
    saved_gate = gaussian(seeds[2], (REPS, GROUP_TOK, FF), 1.0, 6.0, ((0, 2), (1, 4), (2, 16)))
    saved_up = gaussian(seeds[3], (REPS, GROUP_TOK, FF), 1.0, 6.0, ((0, 2), (1, 4), (2, 16)))
    saved_codes = draw_saved_codes(jax.random.fold_in(seeds[6], 71), 0)
    exponents = touch_ends(jax.random.randint(seeds[5], (REPS, GROUP_TOK, FF // BLOCK), -12, -8), jax.random.fold_in(seeds[5], 1), -12, (-8) - 1).astype(jnp.int32)
    return {"grad_out": grad_out, "down_weight": down_weight, "saved_gate": saved_gate, "saved_up": saved_up, "saved_codes": saved_codes, "exponents": exponents}


def sylvester(order):
    indices = jnp.arange(order, dtype=jnp.int32)
    both = jnp.bitwise_and(indices[:, None], indices[None, :])
    parity = jnp.zeros((order, order), jnp.int32)
    for bit_index in range(order.bit_length() - 1):
        parity = jnp.bitwise_xor(parity, jnp.bitwise_and(jnp.right_shift(both, bit_index), 1))
    return (1 - 2 * parity).astype(jnp.float32)

def reference(grad_out, down_weight, saved_gate, saved_up, saved_codes, exponents):
    tokens_all = REPS * GROUP_TOK
    out_flat = grad_out.reshape(tokens_all, D)
    codes_flat = saved_codes.reshape(tokens_all, FF)
    scales = jnp.exp2(exponents.reshape(tokens_all, FF // BLOCK).astype(jnp.float32))
    dequant = (codes_flat.astype(jnp.float32).reshape(tokens_all, FF // BLOCK, BLOCK) * scales[:, :, None]).reshape(tokens_all, FF).astype(jnp.bfloat16)
    width_part = D // SLICES
    grad_quant = jnp.zeros((tokens_all, FF), jnp.float32)
    for column_block in range(SLICES):
        lower = column_block * width_part
        partial_sum = lax.dot_general(out_flat[:, lower:lower + width_part], down_weight[:, lower:lower + width_part], (((1,), (1,)), ((), ())), preferred_element_type=jnp.float32)
        grad_quant = grad_quant + lax.optimization_barrier(partial_sum.astype(jnp.bfloat16)).astype(jnp.float32)
    keep_mask = (codes_flat > -128) & (codes_flat < 127)
    masked = jnp.where(keep_mask, grad_quant, jnp.float32(0.0))
    table_block = sylvester(BLOCK) / math.sqrt(BLOCK)
    table_group = sylvester(GROUPS) / math.sqrt(GROUPS)
    shaped = masked.reshape(tokens_all, GROUPS, FF // GROUPS // BLOCK, BLOCK)
    shaped = jnp.einsum('tgbk,kj->tgbj', shaped, table_block, precision=lax.Precision.HIGHEST)
    shaped = jnp.einsum('tgbj,ge->tebj', shaped, table_group, precision=lax.Precision.HIGHEST)
    grad_hidden = shaped.reshape(tokens_all, FF)
    gate_full = saved_gate.reshape(tokens_all, FF).astype(jnp.float32)
    up_full = saved_up.reshape(tokens_all, FF).astype(jnp.float32)
    sigmoid_gate = jax.nn.sigmoid(gate_full)
    grad_gate = (grad_hidden * up_full * sigmoid_gate * (1.0 + gate_full * (1.0 - sigmoid_gate))).astype(jnp.bfloat16)
    grad_up = (grad_hidden * gate_full * sigmoid_gate).astype(jnp.bfloat16)
    grad_down = jnp.zeros((FF, D), jnp.float32)
    for replica in range(REPS):
        lower = replica * GROUP_TOK
        partial_sum = lax.dot_general(dequant[lower:lower + GROUP_TOK], out_flat[lower:lower + GROUP_TOK], (((0,), (0,)), ((), ())), preferred_element_type=jnp.float32)
        grad_down = grad_down + lax.optimization_barrier(partial_sum.astype(jnp.bfloat16)).astype(jnp.float32)
    return (grad_gate.reshape(REPS, GROUP_TOK, FF), grad_up.reshape(REPS, GROUP_TOK, FF), grad_down)
```

```python
import functools
import math

import jax
import jax.numpy as jnp
from jax import lax
from jax.experimental import pallas as pl
from jax.experimental.pallas import tpu as pltpu
from jax.sharding import PartitionSpec as P

BLOCK = 128
SPLITS = 2
AXES = ("hid", "wid", "rep")
F32 = jnp.float32
BF16 = jnp.bfloat16


def send(value, target):
    route = []
    for hid in range(16):
        for wid in range(4):
            for rep in range(2):
                to_hid, to_wid, to_rep = target(hid, wid, rep)
                route.append((hid * 8 + wid * 2 + rep, to_hid * 8 + to_wid * 2 + to_rep))
    return lax.ppermute(value, AXES, route)


def to_mate(hid, wid, rep):
    return hid, wid ^ 1, rep


def to_pair(hid, wid, rep):
    return hid, wid ^ 2, rep


def to_next(hid, wid, rep):
    return hid, wid ^ 2, rep ^ 1


def to_rep(hid, wid, rep):
    return hid, wid, rep ^ 1


def stage_bit(stage, core):
    return (stage + 2 * core) % 4


def to_stage(stage):
    return lambda hid, wid, rep: (hid ^ (1 << stage_bit(stage, wid & 1)), wid, rep)


def sylvester(order):
    indices = jnp.arange(order, dtype=jnp.int32)
    both = jnp.bitwise_and(indices[:, None], indices[None, :])
    parity = jnp.zeros((order, order), jnp.int32)
    for bit_index in range(order.bit_length() - 1):
        parity = jnp.bitwise_xor(parity, jnp.bitwise_and(jnp.right_shift(both, bit_index), 1))
    return (1 - 2 * parity).astype(F32)


VMEM_SPEC = pl.BlockSpec(memory_space=pltpu.VMEM)
ANY_SPEC = pl.BlockSpec(memory_space=pl.ANY)


def dequant_kernel(codes_ref, scales_ref, out_ref):
    blocks = codes_ref.shape[1] // BLOCK
    for b in range(blocks):
        cols = pl.ds(b * BLOCK, BLOCK)
        part = codes_ref[:, cols].astype(F32) * scales_ref[:, b:b + 1]
        out_ref[cols, :] = part.T.astype(BF16)


def dequant_t(codes, scales):
    tokens, hidden = codes.shape
    return pl.pallas_call(
        dequant_kernel,
        out_shape=jax.ShapeDtypeStruct((hidden, tokens), BF16),
        in_specs=[VMEM_SPEC, VMEM_SPEC],
        out_specs=VMEM_SPEC,
        name="dequant",
    )(codes, scales)


def grad_quant_kernel(order_ref, rows_ref, w_ref, away_ref, keep_ref, lhs_ref, sem, *, part, tokens):
    @pl.when(pl.program_id(0) == 0)
    def _():
        copies = []
        for i in range(4):
            start = pl.multiple_of(order_ref[i] * (tokens * SPLITS) + part * tokens, 128)
            copies.append(pltpu.make_async_copy(
                rows_ref.at[pl.ds(start, tokens)], lhs_ref.at[pl.ds(i * tokens, tokens)], sem.at[i]))
        for copy in copies:
            copy.start()
        for copy in copies:
            copy.wait()
    out = lax.dot_general(lhs_ref[...], w_ref[...], (((1,), (1,)), ((), ())), preferred_element_type=F32).astype(BF16)
    away_ref[...] = out[:2 * tokens]
    keep_ref[...] = out[2 * tokens:]


def grad_quant(order, rows, weight, part):
    total, width = rows.shape
    hidden = weight.shape[0]
    tokens = total // 4 // SPLITS
    tile = 256
    spec = pl.BlockSpec((2 * tokens, tile), lambda i, order: (0, i))
    return pl.pallas_call(
        functools.partial(grad_quant_kernel, part=part, tokens=tokens),
        out_shape=[jax.ShapeDtypeStruct((2 * tokens, hidden), BF16)] * 2,
        grid_spec=pltpu.PrefetchScalarGridSpec(
            num_scalar_prefetch=1,
            grid=(hidden // tile,),
            in_specs=[ANY_SPEC, pl.BlockSpec((tile, width), lambda i, order: (i, 0))],
            out_specs=[spec, spec],
            scratch_shapes=[pltpu.VMEM((4 * tokens, width), BF16), pltpu.SemaphoreType.DMA((4,))],
        ),
        compiler_params=pltpu.CompilerParams(dimension_semantics=("arbitrary",)),
        name="grad_quant",
    )(order, rows, weight)


def rotate_kernel(keep_ref, near_ref, far_ref, codes_ref, table_ref, out_ref, *, scale):
    tokens, hidden = far_ref.shape
    for b in range(hidden // BLOCK):
        cols = pl.ds(b * BLOCK, BLOCK)
        total = keep_ref[:, cols].astype(F32) + near_ref[:, cols].astype(F32) + far_ref[:, cols].astype(F32)
        codes = codes_ref[:, cols]
        masked = jnp.where((codes > -128) & (codes < 127), total, 0.0).astype(BF16)
        mixed = jnp.dot(masked, table_ref[...], preferred_element_type=F32)
        out_ref[:, cols] = (mixed * scale).astype(BF16)


def rotate(keep, near, far, codes, part, table, scale):
    tokens, hidden = far.shape
    whole = pl.BlockSpec((tokens, hidden), lambda i: (0, 0))
    return pl.pallas_call(
        functools.partial(rotate_kernel, scale=scale),
        out_shape=jax.ShapeDtypeStruct((tokens, hidden), BF16),
        grid=(1,),
        in_specs=[whole, whole, whole, pl.BlockSpec((tokens, hidden), lambda i: (part, 0)),
                  pl.BlockSpec((BLOCK, BLOCK), lambda i: (0, 0))],
        out_specs=whole,
        name="rotate",
    )(keep, near, far, codes, table)


def finish_kernel(sign_ref, mine_ref, other_ref, gate_ref, up_ref, *refs):
    gate_out, up_out = refs[-2:]
    for b in range(mine_ref.shape[1] // BLOCK):
        cols = pl.ds(b * BLOCK, BLOCK)
        hidden = other_ref[:, cols].astype(F32) + sign_ref[0] * mine_ref[:, cols].astype(F32)
        gate = gate_ref[:, cols].astype(F32)
        up = up_ref[:, cols].astype(F32)
        sig = 1.0 / (1.0 + jnp.exp(-gate))
        gate_out[:, cols] = (hidden * up * sig * (1.0 + gate * (1.0 - sig))).astype(BF16)
        up_out[:, cols] = (hidden * gate * sig).astype(BF16)


def finish(sign, mine, other, gate, up, part, before):
    tokens, hidden = mine.shape
    whole = pl.BlockSpec((tokens, hidden), lambda i: (0, 0))
    slab = pl.BlockSpec((tokens, hidden), lambda i: (part, 0))
    return pl.pallas_call(
        finish_kernel,
        out_shape=[jax.ShapeDtypeStruct(gate.shape, BF16)] * 2,
        grid=(1,),
        in_specs=[pl.BlockSpec(memory_space=pltpu.SMEM), whole, whole, slab, slab] + [ANY_SPEC] * len(before),
        out_specs=[slab, slab],
        input_output_aliases={5 + i: i for i in range(len(before))},
        name="finish",
    )(sign, mine, other, gate, up, *before)


def down_own_kernel(order_ref, p0, p1, p2, p3, rows_ref, out_ref, rhs_ref, sem):
    @pl.when(pl.program_id(0) == 0)
    def _():
        cols = pl.multiple_of(order_ref[4], 128)
        copies = []
        for i in range(4):
            start = pl.multiple_of(order_ref[i] * 256, 256)
            copies.append(pltpu.make_async_copy(
                rows_ref.at[pl.ds(start, 256), pl.ds(cols, rhs_ref.shape[2])], rhs_ref.at[i], sem.at[i]))
        for copy in copies:
            copy.start()
        for copy in copies:
            copy.wait()
    total = jnp.dot(p0[...], rhs_ref[0], preferred_element_type=F32)
    for i, piece in ((1, p1), (2, p2), (3, p3)):
        total += jnp.dot(piece[...], rhs_ref[i], preferred_element_type=F32)
    out_ref[...] = total.astype(BF16)


def down_own(order, pieces, rows, width):
    hidden, tokens = pieces[0].shape
    tile = 256
    piece = pl.BlockSpec((tile, tokens), lambda i, order: (i, 0))
    return pl.pallas_call(
        down_own_kernel,
        out_shape=jax.ShapeDtypeStruct((hidden, width), BF16),
        grid_spec=pltpu.PrefetchScalarGridSpec(
            num_scalar_prefetch=1,
            grid=(hidden // tile,),
            in_specs=[piece] * 4 + [ANY_SPEC],
            out_specs=pl.BlockSpec((tile, width), lambda i, order: (i, 0)),
            scratch_shapes=[pltpu.VMEM((4, tokens, width), BF16), pltpu.SemaphoreType.DMA((4,))],
        ),
        compiler_params=pltpu.CompilerParams(dimension_semantics=("arbitrary",)),
        name="down_own",
    )(order, *pieces, rows)


def down_far_kernel(order_ref, p0, p1, p2, p3, own_ref, g0, g1, g23, out_ref, rhs_ref, sem):
    @pl.when(pl.program_id(0) == 0)
    def _():
        copies = []
        for i, source in enumerate((g0, g1, g23.at[0], g23.at[1])):
            copies.append(pltpu.make_async_copy(source, rhs_ref.at[order_ref[i]], sem.at[i]))
        for copy in copies:
            copy.start()
        for copy in copies:
            copy.wait()
    total = own_ref[...].astype(F32)
    for i, piece in enumerate((p0, p1, p2, p3)):
        total += jnp.dot(piece[...], rhs_ref[i], preferred_element_type=F32)
    out_ref[...] = total


def down_far(order, pieces, own, g0, g1, g23):
    hidden, tokens = pieces[0].shape
    width = own.shape[1]
    tile = 256
    piece = pl.BlockSpec((tile, tokens), lambda i, order: (i, 0))
    slab = pl.BlockSpec((tile, width), lambda i, order: (i, 0))
    return pl.pallas_call(
        down_far_kernel,
        out_shape=jax.ShapeDtypeStruct((hidden, width), F32),
        grid_spec=pltpu.PrefetchScalarGridSpec(
            num_scalar_prefetch=1,
            grid=(hidden // tile,),
            in_specs=[piece] * 4 + [slab] + [ANY_SPEC] * 3,
            out_specs=slab,
            scratch_shapes=[pltpu.VMEM((4, tokens, width), BF16), pltpu.SemaphoreType.DMA((4,))],
        ),
        compiler_params=pltpu.CompilerParams(dimension_semantics=("arbitrary",)),
        name="down_far",
    )(order, *pieces, own, g0, g1, g23)


def shards(grad_out, down_weight, saved_gate, saved_up, saved_codes, exponents):
    rows = grad_out[0]
    codes = saved_codes[0]
    gate = saved_gate[0]
    up = saved_up[0]
    tokens, hidden = codes.shape
    half = rows.shape[1] // 2
    hid = lax.axis_index("hid")
    wid = lax.axis_index("wid")
    rep = lax.axis_index("rep")
    core = wid & 1

    quarter = ((hid >> 2) & 1) * 2 + (hid & 1)
    g0 = lax.dynamic_slice(rows, (quarter * tokens, (1 - rep) * half), (tokens, half))
    g0 = send(g0, to_rep)
    g1 = send(g0, lambda h, w, r: (h ^ (1 if w & 1 == 0 else 4), w, r))
    g23 = send(jnp.stack([g0, g1]), lambda h, w, r: (h ^ (4 if w & 1 == 0 else 1), w, r))
    first = 1 + core

    scales = jnp.exp2(exponents[0].astype(F32))
    own = dequant_t(codes, scales)
    own_mate = send(own, to_mate)

    table = sylvester(BLOCK).astype(BF16)
    scale = 1.0 / math.sqrt(BLOCK * 16)
    order = jnp.stack([wid ^ 1, wid ^ 3, wid, wid ^ 2]).astype(jnp.int32)
    tok = tokens // SPLITS
    mixed = []
    for part in range(SPLITS):
        away, keep = grad_quant(order, rows, down_weight, part)
        near = send(away, to_mate)
        far = (keep[tok:].astype(F32) + near[tok:].astype(F32)).astype(BF16)
        far = send(far, to_pair)
        mixed.append(rotate(keep, near, far, codes, part, table, scale))

    pair = send(own, to_pair)
    pair_mate = send(pair, to_mate)
    next_ = send(own, to_next)
    next_mate = send(next_, to_mate)
    cross = send(pair, to_next)
    cross_mate = send(cross, to_mate)

    own_order = jnp.stack([wid, wid ^ 1, wid ^ 2, wid ^ 3, rep * half]).astype(jnp.int32)
    down = down_own(own_order, (own, own_mate, pair, pair_mate), rows, half)

    outs = ()
    for part in range(SPLITS):
        mine = mixed[part]
        for stage in range(4):
            other = send(mine, to_stage(stage))
            bit = (stage + 2 * core) % 4
            sign = (1 - 2 * ((hid >> bit) & 1)).astype(F32)
            if stage < 3:
                mine = (other.astype(F32) + sign * mine.astype(F32)).astype(BF16)
        outs = finish(sign[None], mine, other, gate, up, part, outs)

    slots = 2 ^ wid ^ jnp.stack([quarter, quarter ^ first, quarter ^ (3 - first), quarter ^ 3])
    grad_down = down_far(slots.astype(jnp.int32), (next_, next_mate, cross, cross_mate), down, g0, g1, g23)
    return outs[0][None], outs[1][None], grad_down


def solution(mesh):
    in_specs = (
        P("rep", None, "wid"),
        P("hid", "wid"),
        P("rep", "wid", "hid"),
        P("rep", "wid", "hid"),
        P("rep", "wid", "hid"),
        P("rep", "wid", "hid"),
    )
    out_specs = (P("rep", "wid", "hid"), P("rep", "wid", "hid"), P("hid", ("wid", "rep")))
    return jax.shard_map(shards, mesh=mesh, in_specs=in_specs, out_specs=out_specs, check_vma=False)
```

```python
import functools
import math

import jax
import jax.numpy as jnp
from jax import lax
from jax.experimental import pallas as pl
from jax.experimental.pallas import tpu as pltpu
from jax.sharding import PartitionSpec as P


BLOCK = 128
TILE = 256
PARTS = ((0, 1792),)
AXES = ("hid", "wid", "rep")
F32 = jnp.float32
BF16 = jnp.bfloat16
ANY_SPEC = pl.BlockSpec(memory_space=pl.ANY)


def send(value, target):
    route = []
    for hid in range(16):
        for wid in range(4):
            for rep in range(2):
                to_hid, to_wid, to_rep = target(hid, wid, rep)
                route.append((hid * 8 + wid * 2 + rep, to_hid * 8 + to_wid * 2 + to_rep))
    return lax.ppermute(value, AXES, route)


def to_mate(hid, wid, rep):
    return hid, wid ^ 1, rep


def to_pair(hid, wid, rep):
    return hid, wid ^ 2, rep


def to_next(hid, wid, rep):
    return hid, wid ^ 2, rep ^ 1


def to_rep(hid, wid, rep):
    return hid, wid, rep ^ 1


def along(axis, step):
    return lambda hid, wid, rep: (hid ^ (step << 2 * ((wid & 1) ^ axis)), wid, rep)


def place(axis):
    hid = lax.axis_index("hid")
    return jnp.where(lax.axis_index("wid") & 1 == axis, hid, hid >> 2) & 3


def dequant_kernel(codes_ref, exponents_ref, out_ref):
    step = pl.program_id(0)
    blocks = out_ref.shape[0] // BLOCK
    for half in range(blocks):
        drop = -exponents_ref[step * blocks + half]
        scale = jnp.where(drop & 1 == 1, 0.5, 1.0) * jnp.where(drop & 2 == 2, 0.25, 1.0)
        scale = scale * jnp.where(drop & 4 == 4, 2.0 ** -4, 1.0) * jnp.where(drop & 8 == 8, 2.0 ** -8, 1.0)
        span = pl.ds(half * BLOCK, BLOCK)
        out_ref[span, :] = (codes_ref[:, span].astype(F32).T * scale).astype(BF16)


def dequant_t(codes, exponents_t):
    tokens, hidden = codes.shape
    tile = hidden // 2
    return pl.pallas_call(
        dequant_kernel,
        out_shape=jax.ShapeDtypeStruct((hidden, tokens), BF16),
        grid=(hidden // tile,),
        in_specs=[pl.BlockSpec((tokens, tile), lambda i: (0, i)), pl.BlockSpec(exponents_t.shape, lambda i: (0, 0, 0))],
        out_specs=pl.BlockSpec((tile, tokens), lambda i: (i, 0)),
        compiler_params=pltpu.CompilerParams(vmem_limit_bytes=12 << 20),
        name="dequant",
    )(codes, exponents_t)


def grad_quant_kernel(rows_ref, w_ref, far_away, far_keep, near_away, near_keep, total_ref):
    tokens = far_away.shape[0]
    wid = lax.axis_index("wid")
    total_ref[...] = lax.dot_general(
        rows_ref[...], w_ref[...], (((1,), (1,)), ((), ())), preferred_element_type=F32).astype(BF16)
    for flip, out in ((3, far_away), (2, far_keep), (1, near_away), (0, near_keep)):
        out[...] = total_ref[pl.ds(pl.multiple_of((wid ^ flip) * tokens, tokens), tokens), :]


def grad_quant(rows, weight, first, count):
    total, width = rows.shape
    tokens = total // 4
    return pl.pallas_call(
        grad_quant_kernel,
        out_shape=[jax.ShapeDtypeStruct((tokens, count), BF16)] * 4,
        grid=(count // TILE,),
        in_specs=[pl.BlockSpec((total, width), lambda i: (0, 0)),
                  pl.BlockSpec((TILE, width), lambda i: (i + first // TILE, 0))],
        out_specs=[pl.BlockSpec((tokens, TILE), lambda i: (0, i))] * 4,
        scratch_shapes=[pltpu.VMEM((total, TILE), BF16)],
        name="grad_quant",
    )(rows, weight)


SMALL = pltpu.CompilerParams(vmem_limit_bytes=12 << 20)
VMEM_SPEC = pl.BlockSpec(memory_space=pltpu.VMEM)


def rotate_kernel(*refs, scale, parts):
    codes_ref = refs[3 * len(parts)]
    outs = refs[3 * len(parts) + 1:]
    rows = outs[0].shape[0]
    mine = place(0)
    row = lax.broadcasted_iota(jnp.int32, (TILE, TILE), 0)
    col = lax.broadcasted_iota(jnp.int32, (TILE, TILE), 1)
    bits = row & col & (BLOCK - 1)
    for shift in (4, 2, 1):
        bits = bits ^ (bits >> shift)
    sign = (1 - 2 * (bits & 1)).astype(F32)
    table = jnp.where((row ^ col) < BLOCK, sign, 0.0).astype(BF16)
    for part, (start, count) in enumerate(parts):
        keep_ref, away_ref, far_ref = refs[3 * part:3 * part + 3]
        for first in range(0, count, TILE):
            here = pl.ds(first, TILE)
            cols = pl.ds(start + first, TILE)
            total = keep_ref[:, here].astype(F32) + away_ref[:, here].astype(F32) + far_ref[:, here].astype(F32)
            codes = codes_ref[:, cols]
            masked = jnp.where((codes > -128) & (codes < 127), total, 0.0).astype(BF16)
            mixed = (jnp.dot(masked, table, preferred_element_type=F32) * scale).astype(BF16)
            for quarter in range(4):
                piece = mixed[quarter * rows:(quarter + 1) * rows]
                for step, out in enumerate(outs):
                    @pl.when(mine ^ step == quarter)
                    def _():
                        out[:, cols] = piece


def rotate(sums, codes, scale):
    tokens, hidden = codes.shape
    return pl.pallas_call(
        functools.partial(rotate_kernel, scale=scale, parts=PARTS),
        out_shape=[pltpu.VMEM((tokens // 4, hidden), BF16)] * 4,
        in_specs=[VMEM_SPEC] * (3 * len(PARTS) + 1),
        out_specs=[VMEM_SPEC] * 4,
        compiler_params=SMALL,
        name="rotate",
    )(*[value for group in sums for value in group], codes)


def parity(value):
    return (1 - 2 * ((value ^ (value >> 1)) & 1)).astype(F32)


def mix_kernel(*refs, axis):
    mine = place(axis)
    signs = [parity(mine & step) for step in range(4)]
    whole = parity(mine)
    hidden = refs[0].shape[1]
    for first in range(0, hidden, TILE):
        cols = pl.ds(first, TILE)
        p0, p1, p2, p3 = [refs[step][:, cols].astype(F32) * signs[step] for step in range(4)]
        even, odd = (p0 + p1, p2 + p3), (p0 - p1, p2 - p3)
        outs = (even[0] + even[1], odd[0] + odd[1], even[0] - even[1], odd[0] - odd[1])
        for step in range(4):
            refs[4 + step][:, cols] = (outs[step] * (whole * signs[step])).astype(BF16)


def relabel_kernel(*refs):
    turn = place(0) ^ place(1)
    for step in range(4):
        for other in range(4):
            @pl.when(turn == step ^ other)
            def _():
                refs[4 + step][...] = refs[other][...]


def four(kernel, pieces):
    return pl.pallas_call(
        kernel,
        out_shape=[pltpu.VMEM(pieces[0].shape, BF16)] * 4,
        in_specs=[VMEM_SPEC] * 4,
        out_specs=[VMEM_SPEC] * 4,
        compiler_params=SMALL,
    )(*pieces)


def finish_kernel(p0, p1, p2, p3, gate_ref, up_ref, gate_out, up_out):
    mine = place(1)
    rows = p0.shape[0]
    for step, piece in enumerate((p0, p1, p2, p3)):
        span = pl.ds(pl.multiple_of((mine ^ step) * rows, rows), rows)
        for first in range(0, piece.shape[1], TILE):
            cols = pl.ds(first, TILE)
            hidden = piece[:, cols].astype(F32)
            gate = gate_ref[span, cols].astype(F32)
            up = up_ref[span, cols].astype(F32)
            sig = jax.nn.sigmoid(gate)
            gate_out[span, cols] = (hidden * up * sig * (1.0 + gate * (1.0 - sig))).astype(BF16)
            up_out[span, cols] = (hidden * gate * sig).astype(BF16)


def finish(pieces, gate, up):
    return pl.pallas_call(
        finish_kernel,
        out_shape=[jax.ShapeDtypeStruct(gate.shape, BF16)] * 2,
        in_specs=[VMEM_SPEC] * 6,
        out_specs=[VMEM_SPEC] * 2,
        compiler_params=SMALL,
        name="finish",
    )(*pieces, gate, up)


def down_kernel(*refs, flips, remote, summed):
    count = len(flips)
    pieces, sources = refs[:count], refs[count:-4 - summed]
    out_ref, lhs_ref, rhs_ref, sem = refs[-4:]
    tokens = pieces[0].shape[1]
    width = rhs_ref.shape[1]
    step = pl.program_id(0)
    cols = pl.ds(pl.multiple_of(step * TILE, TILE), TILE)

    def store(total):
        if summed:
            total = total + refs[-5][...].astype(F32)
        out_ref[...] = total.astype(out_ref.dtype)

    @pl.when(step == 0)
    def _():
        hid = lax.axis_index("hid")
        wid = lax.axis_index("wid")
        first_col = pl.multiple_of(lax.axis_index("rep") * width, width)
        quarter = ((hid >> 2) & 1) * 2 + (hid & 1)
        left = [pltpu.make_async_copy(piece, lhs_ref.at[:, pl.ds(i * tokens, tokens)], sem.at[i])
                for i, piece in enumerate(pieces)]
        right = []
        for i, flip in enumerate(flips):
            left[i].start()
            target = rhs_ref.at[pl.ds(i * tokens, tokens)]
            if not remote:
                span = pl.ds(pl.multiple_of((wid ^ flip) * tokens, tokens), tokens)
                right.append(pltpu.make_async_copy(sources[0].at[span, pl.ds(first_col, width)], target, sem.at[count + i]))
                right[i].start()
                continue
            g0, g1, g23 = sources
            where = quarter ^ wid ^ flip
            index = jnp.where(wid & 1 == 0, where, (where >> 1) | ((where & 1) << 1))
            for number, source in enumerate((g0, g1, g23.at[0], g23.at[1])):
                @pl.when(index == number)
                def _():
                    pltpu.make_async_copy(source, target, sem.at[count + i]).start()
            right.append(pltpu.make_async_copy(g0, target, sem.at[count + i]))
        total = None
        for i in range(count):
            left[i].wait()
            right[i].wait()
            part = jnp.dot(lhs_ref[:, i * tokens:(i + 1) * tokens], rhs_ref[i * tokens:(i + 1) * tokens, :TILE],
                           preferred_element_type=F32)
            total = part if total is None else total + part
        store(total)

    @pl.when(step > 0)
    def _():
        store(jnp.dot(lhs_ref[...], rhs_ref[:, cols], preferred_element_type=F32))


def down(pieces, flips, sources, width, acc=None, dtype=BF16):
    hidden, tokens = pieces[0].shape
    count = len(pieces)
    spec = pl.BlockSpec((hidden, TILE), lambda i: (0, i))
    return pl.pallas_call(
        functools.partial(down_kernel, flips=flips, remote=len(sources) > 1, summed=acc is not None),
        out_shape=jax.ShapeDtypeStruct((hidden, width), dtype),
        grid=(width // TILE,),
        in_specs=[ANY_SPEC] * (count + len(sources)) + [spec] * (acc is not None),
        out_specs=spec,
        scratch_shapes=[pltpu.VMEM((hidden, count * tokens), BF16), pltpu.VMEM((count * tokens, width), BF16),
                        pltpu.SemaphoreType.DMA((2 * count,))],
        name="down",
    )(*pieces, *sources, *(() if acc is None else (acc,)))


def shards(grad_out, down_weight, saved_gate, saved_up, saved_codes, exponents):
    rows = grad_out[0]
    codes = saved_codes[0]
    tokens = codes.shape[0]
    half = rows.shape[1] // 2
    hid = lax.axis_index("hid")
    wid = lax.axis_index("wid")
    rep = lax.axis_index("rep")
    core = wid & 1
    scale = 1.0 / math.sqrt(BLOCK * 16)

    quarter = ((hid >> 2) & 1) * 2 + (hid & 1)
    g0 = lax.dynamic_slice(rows, (quarter * tokens, (1 - rep) * half), (tokens, half))
    g0 = send(g0, to_rep)
    g1 = send(g0, lambda h, w, r: (h ^ (3 if w & 1 == 0 else 12), w, r))
    g23 = send(jnp.stack([g0, g1]), lambda h, w, r: (h ^ (12 if w & 1 == 0 else 3), w, r))
    others = (g0, g1, g23)

    own = dequant_t(codes, jnp.transpose(exponents, (2, 0, 1)))
    own_mate = send(own, to_mate)
    next_ = send(own, to_next)
    next_mate = send(next_, to_mate)

    sums = []
    for first, count in PARTS:
        far_away, far_keep, near_away, near_keep = grad_quant(rows, down_weight, first, count)
        far_away = send(far_away, to_mate)
        near_away = send(near_away, to_mate)
        far = (far_keep.astype(F32) + far_away.astype(F32)).astype(BF16)
        far = send(far, to_pair)
        sums.append((near_keep, near_away, far))

    pair = send(own, to_pair)
    pair_mate = send(pair, to_mate)
    cross = jnp.where(core == 0, pair, next_)
    cross = send(cross, lambda h, w, r: (h, w ^ 2, r ^ 1 if w & 1 == 0 else r))
    cross_mate = send(cross, to_mate)

    product = down((own, own_mate), (0, 1), (rows,), half)
    product = down((next_, next_mate), (2, 3), others, half, product)
    product = down((pair, pair_mate), (2, 3), (rows,), half, product)

    def spread(pieces, axis):
        moved = list(pieces)
        for step in (2, 1, 3):
            moved[step] = send(pieces[step], along(axis, step))
        return moved

    pieces = rotate(sums, codes, scale)
    pieces = spread(pieces, 0)
    pieces = four(functools.partial(mix_kernel, axis=0), pieces)
    pieces = spread(pieces, 0)
    pieces = four(relabel_kernel, pieces)
    pieces = spread(pieces, 1)
    pieces = four(functools.partial(mix_kernel, axis=1), pieces)
    pieces = spread(pieces, 1)
    grad_gate, grad_up = finish(pieces, saved_gate[0], saved_up[0])

    grad_down = down((cross, cross_mate), (0, 1), others, half, product, F32)
    return grad_gate[None], grad_up[None], grad_down


def solution(mesh):
    in_specs = (
        P("rep", None, "wid"),
        P("hid", "wid"),
        P("rep", "wid", "hid"),
        P("rep", "wid", "hid"),
        P("rep", "wid", "hid"),
        P("rep", "wid", "hid"),
    )
    out_specs = (P("rep", "wid", "hid"), P("rep", "wid", "hid"), P("hid", ("wid", "rep")))


    return jax.shard_map(shards, mesh=mesh, in_specs=in_specs, out_specs=out_specs, check_vma=False)
```

```python
import functools
import math

import jax
import jax.numpy as jnp
from jax import lax
from jax.experimental import pallas as pl
from jax.experimental.pallas import tpu as pltpu
from jax.sharding import PartitionSpec as P


BLOCK = 128
TILE = 256
PARTS = ((0, 1024), (1024, 768))
AXES = ("hid", "wid", "rep")
F32 = jnp.float32
BF16 = jnp.bfloat16
ANY_SPEC = pl.BlockSpec(memory_space=pl.ANY)
VMEM_SPEC = pl.BlockSpec(memory_space=pltpu.VMEM)
SMALL = pltpu.CompilerParams(vmem_limit_bytes=12 << 20)


def send(value, target):
    route = []
    for hid in range(16):
        for wid in range(4):
            for rep in range(2):
                to_hid, to_wid, to_rep = target(hid, wid, rep)
                route.append((hid * 8 + wid * 2 + rep, to_hid * 8 + to_wid * 2 + to_rep))
    return lax.ppermute(value, AXES, route)


def to_mate(hid, wid, rep):
    return hid, wid ^ 1, rep


def to_pair(hid, wid, rep):
    return hid, wid ^ 2, rep


def to_next(hid, wid, rep):
    return hid, wid ^ 2, rep ^ 1


def to_rep(hid, wid, rep):
    return hid, wid, rep ^ 1


def along(axis, step):
    return lambda hid, wid, rep: (hid ^ (step << 2 * ((wid & 1) ^ axis)), wid, rep)


def place(axis):
    hid = lax.axis_index("hid")
    return jnp.where(lax.axis_index("wid") & 1 == axis, hid, hid >> 2) & 3


def dequant_kernel(codes_ref, exponents_ref, out_ref):
    step = pl.program_id(0)
    blocks = codes_ref.shape[1] // BLOCK
    for half in range(blocks):
        drop = -exponents_ref[step * blocks + half]
        scale = jnp.where(drop & 1 == 1, 0.5, 1.0) * jnp.where(drop & 2 == 2, 0.25, 1.0)
        scale = scale * jnp.where(drop & 4 == 4, 2.0 ** -4, 1.0) * jnp.where(drop & 8 == 8, 2.0 ** -8, 1.0)
        span = pl.ds(half * BLOCK, BLOCK)
        out_ref[pl.ds(pl.multiple_of((step * blocks + half) * BLOCK, BLOCK), BLOCK), :] = (codes_ref[:, span].astype(F32).T * scale).astype(BF16)


def dequant_t(codes, exponents_t):
    tokens, hidden = codes.shape
    tile = hidden // 2
    return pl.pallas_call(
        dequant_kernel,
        out_shape=pltpu.VMEM((hidden, tokens), BF16),
        grid=(hidden // tile,),
        in_specs=[pl.BlockSpec((tokens, tile), lambda i: (0, i)), pl.BlockSpec(exponents_t.shape, lambda i: (0, 0, 0))],
        out_specs=pl.BlockSpec(memory_space=pltpu.VMEM),
        compiler_params=pltpu.CompilerParams(vmem_limit_bytes=12 << 20),
        name="dequant",
    )(codes, exponents_t)


CONTRACT = (((1,), (1,)), ((), ()))


def scatter_rows(total_ref, outs, first):
    tokens = outs[0].shape[0]
    wid = lax.axis_index("wid")
    cols = pl.ds(pl.multiple_of(first, TILE), TILE)
    for flip, out in zip((3, 2, 1, 0), outs):
        out[:, cols] = total_ref[pl.ds(pl.multiple_of((wid ^ flip) * tokens, tokens), tokens), :]


def first_product_kernel(rows_ref, w_ref, *refs):
    outs, (rows_out, w_out, w_buf, total_ref, rows_sem, w_sem, rest_sem) = refs[:4], refs[4:]
    count = outs[0].shape[1]
    chunk = rows_ref.shape[0] // 4

    def weights(tile):
        span = pl.ds(pl.multiple_of(tile * TILE, TILE), TILE)
        return pltpu.make_async_copy(w_ref.at[span], w_buf.at[span], w_sem.at[tile])

    rows = [pltpu.make_async_copy(rows_ref.at[pl.ds(i * chunk, chunk)], rows_out.at[pl.ds(i * chunk, chunk)], rows_sem.at[i])
            for i in range(4)]
    rest = pltpu.make_async_copy(w_ref.at[pl.ds(count, w_out.shape[0])], w_out, rest_sem)
    weights(0).start()
    for copy in rows:
        copy.start()
    for tile in range(1, count // TILE):
        weights(tile).start()
    rest.start()
    for copy in rows:
        copy.wait()

    def body(tile, carry):
        weights(tile).wait()
        span = pl.ds(pl.multiple_of(tile * TILE, TILE), TILE)
        total_ref[...] = lax.dot_general(
            rows_out[...], w_buf[span, :], CONTRACT, preferred_element_type=F32).astype(BF16)
        scatter_rows(total_ref, outs, tile * TILE)
        return carry

    lax.fori_loop(0, count // TILE, body, 0)
    rest.wait()


def first_product(rows, weight, count):
    total, width = rows.shape
    hbm = pl.BlockSpec(memory_space=pltpu.HBM)
    return pl.pallas_call(
        first_product_kernel,
        out_shape=[pltpu.VMEM((total // 4, count), BF16)] * 4
        + [pltpu.VMEM((total, width), BF16), pltpu.VMEM((weight.shape[0] - count, width), BF16)],
        in_specs=[hbm, hbm],
        out_specs=[VMEM_SPEC] * 6,
        scratch_shapes=[pltpu.VMEM((count, width), BF16), pltpu.VMEM((total, TILE), BF16), pltpu.SemaphoreType.DMA((4,)),
                        pltpu.SemaphoreType.DMA((count // TILE,)), pltpu.SemaphoreType.DMA(())],
        compiler_params=pltpu.CompilerParams(vmem_limit_bytes=52 << 20),
        name="first_product",
    )(rows, weight)


def second_product_kernel(rows_ref, w_ref, *refs):
    outs, total_ref = refs[:4], refs[4]

    def body(tile, carry):
        span = pl.ds(pl.multiple_of(tile * TILE, TILE), TILE)
        total_ref[...] = lax.dot_general(
            rows_ref[...], w_ref[span, :], CONTRACT, preferred_element_type=F32).astype(BF16)
        scatter_rows(total_ref, outs, tile * TILE)
        return carry

    lax.fori_loop(0, outs[0].shape[1] // TILE, body, 0)


def second_product(rows, weight):
    total, count = rows.shape[0], weight.shape[0]
    return pl.pallas_call(
        second_product_kernel,
        out_shape=[pltpu.VMEM((total // 4, count), BF16)] * 4,
        in_specs=[VMEM_SPEC] * 2,
        out_specs=[VMEM_SPEC] * 4,
        scratch_shapes=[pltpu.VMEM((total, TILE), BF16)],
        compiler_params=SMALL,
        name="second_product",
    )(rows, weight)


def small(kernel, operands, shape, spec=None):
    return pl.pallas_call(
        kernel,
        out_shape=pltpu.VMEM(shape, BF16),
        in_specs=[spec or VMEM_SPEC] * len(operands),
        out_specs=VMEM_SPEC,
        scratch_shapes=[pltpu.SemaphoreType.DMA(())] if spec else [],
        compiler_params=pltpu.CompilerParams(vmem_limit_bytes=60 << 20) if spec else SMALL,
    )(*operands)


def quarter_kernel(rows_ref, out_ref, sem):
    hid = lax.axis_index("hid")
    tokens, half = out_ref.shape
    quarter = ((hid >> 2) & 1) * 2 + (hid & 1)
    source = rows_ref.at[pl.ds(pl.multiple_of(quarter * tokens, tokens), tokens),
                         pl.ds(pl.multiple_of((1 - lax.axis_index("rep")) * half, half), half)]
    copy = pltpu.make_async_copy(source, out_ref, sem)
    copy.start()
    copy.wait()


def join_kernel(a_ref, b_ref, out_ref):
    out_ref[...] = (a_ref[...].astype(F32) + b_ref[...].astype(F32)).astype(BF16)


def stack_kernel(a_ref, b_ref, out_ref):
    out_ref[0] = a_ref[...]
    out_ref[1] = b_ref[...]


def choose_kernel(a_ref, b_ref, out_ref):
    core = lax.axis_index("wid") & 1
    for number, source in enumerate((a_ref, b_ref)):
        @pl.when(core == number)
        def _():
            out_ref[...] = source[...]


def rotate_kernel(*refs, scale, parts):
    codes_ref = refs[3 * len(parts)]
    outs, mixed_ref = refs[3 * len(parts) + 1:-1], refs[-1]
    rows = outs[0].shape[0]
    mine = place(0)
    row = lax.broadcasted_iota(jnp.int32, (TILE, TILE), 0)
    col = lax.broadcasted_iota(jnp.int32, (TILE, TILE), 1)
    bits = row & col & (BLOCK - 1)
    for shift in (4, 2, 1):
        bits = bits ^ (bits >> shift)
    sign = (1 - 2 * (bits & 1)).astype(F32)
    table = jnp.where((row ^ col) < BLOCK, sign, 0.0).astype(BF16)
    for part, (start, count) in enumerate(parts):
        keep_ref, away_ref, far_ref = refs[3 * part:3 * part + 3]
        for first in range(0, count, TILE):
            here = pl.ds(first, TILE)
            cols = pl.ds(start + first, TILE)
            total = keep_ref[:, here].astype(F32) + away_ref[:, here].astype(F32) + far_ref[:, here].astype(F32)
            codes = codes_ref[:, cols]
            masked = jnp.where((codes > -128) & (codes < 127), total, 0.0).astype(BF16)
            mixed = jnp.dot(masked, table, preferred_element_type=F32)
            mixed_ref[:, cols] = (mixed * scale).astype(BF16)
    for step, out in enumerate(outs):
        out[...] = mixed_ref[pl.ds(pl.multiple_of((mine ^ step) * rows, rows), rows), :]


def rotate(sums, codes, scale):
    tokens, hidden = codes.shape
    return pl.pallas_call(
        functools.partial(rotate_kernel, scale=scale, parts=PARTS),
        out_shape=[pltpu.VMEM((tokens // 4, hidden), BF16)] * 4,
        in_specs=[VMEM_SPEC] * (3 * len(PARTS) + 1),
        out_specs=[VMEM_SPEC] * 4,
        scratch_shapes=[pltpu.VMEM((tokens, hidden), BF16)],
        compiler_params=SMALL,
        name="rotate",
    )(*[value for group in sums for value in group], codes)


def parity(value):
    return (1 - 2 * ((value ^ (value >> 1)) & 1)).astype(F32)


def mix_kernel(*refs, axis):
    mine = place(axis)
    signs = [parity(mine & step) for step in range(4)]
    whole = parity(mine)
    hidden = refs[0].shape[1]
    for first in range(0, hidden, TILE):
        cols = pl.ds(first, TILE)
        p0, p1, p2, p3 = [refs[step][:, cols].astype(F32) * signs[step] for step in range(4)]
        even, odd = (p0 + p1, p2 + p3), (p0 - p1, p2 - p3)
        outs = (even[0] + even[1], odd[0] + odd[1], even[0] - even[1], odd[0] - odd[1])
        for step in range(4):
            refs[4 + step][:, cols] = (outs[step] * (whole * signs[step])).astype(BF16)


def relabel_kernel(*refs):
    turn = place(0) ^ place(1)
    for step in range(4):
        for other in range(4):
            @pl.when(turn == step ^ other)
            def _():
                refs[4 + step][...] = refs[other][...]


def four(kernel, pieces):
    return pl.pallas_call(
        kernel,
        out_shape=[pltpu.VMEM(pieces[0].shape, BF16)] * 4,
        in_specs=[VMEM_SPEC] * 4,
        out_specs=[VMEM_SPEC] * 4,
        compiler_params=SMALL,
    )(*pieces)


def finish_kernel(p0, p1, p2, p3, gate_ref, up_ref, gate_out, up_out):
    mine = place(1)
    rows = p0.shape[0]
    for step, piece in enumerate((p0, p1, p2, p3)):
        span = pl.ds(pl.multiple_of((mine ^ step) * rows, rows), rows)
        for first in range(0, piece.shape[1], TILE):
            cols = pl.ds(first, TILE)
            hidden = piece[:, cols].astype(F32)
            gate = gate_ref[span, cols].astype(F32)
            up = up_ref[span, cols].astype(F32)
            sig = jax.nn.sigmoid(gate)
            gate_out[span, cols] = (hidden * up * sig * (1.0 + gate * (1.0 - sig))).astype(BF16)
            up_out[span, cols] = (hidden * gate * sig).astype(BF16)


def finish(pieces, gate, up):
    return pl.pallas_call(
        finish_kernel,
        out_shape=[jax.ShapeDtypeStruct(gate.shape, BF16)] * 2,
        in_specs=[VMEM_SPEC] * 6,
        out_specs=[VMEM_SPEC] * 2,
        compiler_params=SMALL,
        name="finish",
    )(*pieces, gate, up)


def arrange_kernel(g0, g1, g23, out_ref):
    hid = lax.axis_index("hid")
    core = lax.axis_index("wid") & 1
    quarter = ((hid >> 2) & 1) * 2 + (hid & 1)
    tokens = g0.shape[0]
    for source, flip in ((g0, 0), (g1, 1 + core), (g23.at[0], 2 - core), (g23.at[1], 3)):
        out_ref[pl.ds(pl.multiple_of((quarter ^ flip) * tokens, tokens), tokens), :] = source[...]


def arrange(g0, g1, g23):
    return pl.pallas_call(
        arrange_kernel,
        out_shape=pltpu.VMEM((4 * g0.shape[0], g0.shape[1]), BF16),
        in_specs=[VMEM_SPEC] * 3,
        out_specs=VMEM_SPEC,
        compiler_params=SMALL,
        name="arrange",
    )(g0, g1, g23)


def down_kernel(*refs, flips, summed, last, mine):
    count = len(flips)
    pieces, rows_ref = refs[:count], refs[count]
    acc_ref = refs[count + 1] if summed else None
    out_ref = refs[count + 1 + summed]
    wid = lax.axis_index("wid")
    tokens = pieces[0].shape[1]
    width = out_ref.shape[1]
    offset = lax.axis_index("rep") * width if mine else 0
    copies = []
    for number, first in enumerate(range(0, width, TILE)):
        cols = pl.ds(first, TILE)
        total = None
        for piece, flip in zip(pieces, flips):
            right = rows_ref[pl.ds(pl.multiple_of((wid ^ flip) * tokens, tokens), tokens),
                             pl.ds(pl.multiple_of(offset + first, TILE), TILE)]
            part = jnp.dot(piece[...], right, preferred_element_type=F32)
            total = part if total is None else total + part
        if summed:
            total = total + acc_ref[:, cols].astype(F32)
        if not last:
            out_ref[:, cols] = total.astype(BF16)
            continue
        buffer_ref, sem = refs[-2:]
        buffer_ref[number] = total
        copies.append(pltpu.make_async_copy(buffer_ref.at[number], out_ref.at[:, cols], sem.at[number]))
        copies[-1].start()
    for copy in copies:
        copy.wait()


def down(pieces, flips, rows, width, acc=None, last=False):
    hidden, _ = pieces[0].shape
    operands = (*pieces, rows) if acc is None else (*pieces, rows, acc)
    scratch = [pltpu.VMEM((width // TILE, hidden, TILE), F32), pltpu.SemaphoreType.DMA((width // TILE,))]
    return pl.pallas_call(
        functools.partial(
            down_kernel, flips=flips, summed=acc is not None, last=last, mine=rows.shape[1] > width),
        out_shape=jax.ShapeDtypeStruct((hidden, width), F32) if last else pltpu.VMEM((hidden, width), BF16),
        in_specs=[VMEM_SPEC] * len(operands),
        out_specs=ANY_SPEC if last else VMEM_SPEC,
        scratch_shapes=scratch if last else [],
        compiler_params=pltpu.CompilerParams(vmem_limit_bytes=24 << 20),
        name="down",
    )(*operands)


def shards(grad_out, down_weight, saved_gate, saved_up, saved_codes, exponents):
    rows = grad_out[0]
    codes = saved_codes[0]
    tokens = codes.shape[0]
    half = rows.shape[1] // 2
    scale = 1.0 / math.sqrt(BLOCK * 16)

    g0 = small(quarter_kernel, (rows,), (tokens, half), pl.BlockSpec(memory_space=pltpu.HBM))
    g0 = send(g0, to_rep)
    g1 = send(g0, lambda h, w, r: (h ^ (3 if w & 1 == 0 else 12), w, r))
    g23 = small(stack_kernel, (g0, g1), (2, tokens, half))
    g23 = send(g23, lambda h, w, r: (h ^ (12 if w & 1 == 0 else 3), w, r))

    own = dequant_t(codes, jnp.transpose(exponents, (2, 0, 1)))
    own_mate = send(own, to_mate)
    next_ = send(own, to_next)
    next_mate = send(next_, to_mate)

    sums = []
    for part, (first, count) in enumerate(PARTS):
        if part == 0:
            far_away, far_keep, near_away, near_keep, rows_near, rest = first_product(rows, down_weight, count)
        else:
            far_away, far_keep, near_away, near_keep = second_product(rows_near, rest)
        far_away = send(far_away, to_mate)
        near_away = send(near_away, to_mate)
        far = small(join_kernel, (far_keep, far_away), far_keep.shape)
        far = send(far, to_pair)
        sums.append((near_keep, near_away, far))

    pair = send(own, to_pair)
    pair_mate = send(pair, to_mate)
    cross = small(choose_kernel, (pair, next_), pair.shape)
    cross = send(cross, lambda h, w, r: (h, w ^ 2, r ^ 1 if w & 1 == 0 else r))
    cross_mate = send(cross, to_mate)

    product = down((own, own_mate), (0, 1), rows_near, half)
    other_rows = arrange(g0, g1, g23)
    product = down((next_, next_mate), (2, 3), other_rows, half, product)
    product = down((pair, pair_mate), (2, 3), rows_near, half, product)

    def spread(pieces, axis):
        moved = list(pieces)
        for step in (2, 1, 3):
            moved[step] = send(pieces[step], along(axis, step))
        return moved

    pieces = rotate(sums, codes, scale)
    pieces = spread(pieces, 0)
    pieces = four(functools.partial(mix_kernel, axis=0), pieces)
    pieces = spread(pieces, 0)
    pieces = four(relabel_kernel, pieces)
    pieces = spread(pieces, 1)
    pieces = four(functools.partial(mix_kernel, axis=1), pieces)
    pieces = spread(pieces, 1)
    grad_gate, grad_up = finish(pieces, saved_gate[0], saved_up[0])

    grad_down = down((cross, cross_mate), (0, 1), other_rows, half, product, last=True)
    return grad_gate[None], grad_up[None], grad_down


def solution(mesh):
    in_specs = (
        P("rep", None, "wid"),
        P("hid", "wid"),
        P("rep", "wid", "hid"),
        P("rep", "wid", "hid"),
        P("rep", "wid", "hid"),
        P("rep", "wid", "hid"),
    )
    out_specs = (P("rep", "wid", "hid"), P("rep", "wid", "hid"), P("hid", ("wid", "rep")))


    return jax.shard_map(shards, mesh=mesh, in_specs=in_specs, out_specs=out_specs, check_vma=False)
```

```python
import functools
import math

import jax
import jax.numpy as jnp
from jax import lax
from jax.experimental import pallas as pl
from jax.experimental.pallas import tpu as pltpu
from jax.sharding import PartitionSpec as P


BLOCK = 128
TILE = 256
PARTS = ((0, 1024), (1024, 768))
AXES = ("hid", "wid", "rep")
F32 = jnp.float32
BF16 = jnp.bfloat16
ANY_SPEC = pl.BlockSpec(memory_space=pl.ANY)
VMEM_SPEC = pl.BlockSpec(memory_space=pltpu.VMEM)
SMALL = pltpu.CompilerParams(vmem_limit_bytes=12 << 20)


def send(value, target):
    route = []
    for hid in range(16):
        for wid in range(4):
            for rep in range(2):
                to_hid, to_wid, to_rep = target(hid, wid, rep)
                route.append((hid * 8 + wid * 2 + rep, to_hid * 8 + to_wid * 2 + to_rep))
    return lax.ppermute(value, AXES, route)


def to_mate(hid, wid, rep):
    return hid, wid ^ 1, rep


def to_pair(hid, wid, rep):
    return hid, wid ^ 2, rep


def to_next(hid, wid, rep):
    return hid, wid ^ 2, rep ^ 1


def to_rep(hid, wid, rep):
    return hid, wid, rep ^ 1


def along(axis, step):
    return lambda hid, wid, rep: (hid ^ (step << 2 * ((wid & 1) ^ axis)), wid, rep)


def place(axis):
    hid = lax.axis_index("hid")
    return jnp.where(lax.axis_index("wid") & 1 == axis, hid, hid >> 2) & 3


def dequant_kernel(codes_ref, exponents_ref, out_ref):
    step = pl.program_id(0)
    blocks = codes_ref.shape[1] // BLOCK
    for half in range(blocks):
        drop = -exponents_ref[step * blocks + half]
        scale = jnp.where(drop & 1 == 1, 0.5, 1.0) * jnp.where(drop & 2 == 2, 0.25, 1.0)
        scale = scale * jnp.where(drop & 4 == 4, 2.0 ** -4, 1.0) * jnp.where(drop & 8 == 8, 2.0 ** -8, 1.0)
        span = pl.ds(half * BLOCK, BLOCK)
        out_ref[pl.ds(pl.multiple_of((step * blocks + half) * BLOCK, BLOCK), BLOCK), :] = (codes_ref[:, span].astype(F32).T * scale).astype(BF16)


def dequant_t(codes, exponents_t):
    tokens, hidden = codes.shape
    tile = hidden // 2
    return pl.pallas_call(
        dequant_kernel,
        out_shape=pltpu.VMEM((hidden, tokens), BF16),
        grid=(hidden // tile,),
        in_specs=[pl.BlockSpec((tokens, tile), lambda i: (0, i)), pl.BlockSpec(exponents_t.shape, lambda i: (0, 0, 0))],
        out_specs=pl.BlockSpec(memory_space=pltpu.VMEM),
        compiler_params=pltpu.CompilerParams(vmem_limit_bytes=12 << 20),
        name="dequant",
    )(codes, exponents_t)


CONTRACT = (((1,), (1,)), ((), ()))


def scatter_rows(total_ref, outs, first):
    tokens = outs[0].shape[0]
    wid = lax.axis_index("wid")
    cols = pl.ds(pl.multiple_of(first, TILE), TILE)
    for flip, out in zip((3, 2, 1, 0), outs):
        out[:, cols] = total_ref[pl.ds(pl.multiple_of((wid ^ flip) * tokens, tokens), tokens), :]


def first_product_kernel(rows_ref, w_ref, *refs):
    outs, (rows_out, w_out, w_buf, total_ref, rows_sem, w_sem, rest_sem) = refs[:4], refs[4:]
    count = outs[0].shape[1]
    chunk = rows_ref.shape[0] // 4

    def weights(tile):
        span = pl.ds(pl.multiple_of(tile * TILE, TILE), TILE)
        return pltpu.make_async_copy(w_ref.at[span], w_buf.at[span], w_sem.at[tile])

    rows = [pltpu.make_async_copy(rows_ref.at[pl.ds(i * chunk, chunk)], rows_out.at[pl.ds(i * chunk, chunk)], rows_sem.at[i])
            for i in range(4)]
    rest = pltpu.make_async_copy(w_ref.at[pl.ds(count, w_out.shape[0])], w_out, rest_sem)
    weights(0).start()
    for copy in rows:
        copy.start()
    for copy in rows:
        copy.wait()
    for tile in range(1, count // TILE):
        weights(tile).start()
    rest.start()

    def body(tile, carry):
        weights(tile).wait()
        span = pl.ds(pl.multiple_of(tile * TILE, TILE), TILE)
        total_ref[...] = lax.dot_general(
            rows_out[...], w_buf[span, :], CONTRACT, preferred_element_type=F32).astype(BF16)
        scatter_rows(total_ref, outs, tile * TILE)
        return carry

    lax.fori_loop(0, count // TILE, body, 0)
    rest.wait()


def first_product(rows, weight, count):
    total, width = rows.shape
    hbm = pl.BlockSpec(memory_space=pltpu.HBM)
    return pl.pallas_call(
        first_product_kernel,
        out_shape=[pltpu.VMEM((total // 4, count), BF16)] * 4
        + [pltpu.VMEM((total, width), BF16), pltpu.VMEM((weight.shape[0] - count, width), BF16)],
        in_specs=[hbm, hbm],
        out_specs=[VMEM_SPEC] * 6,
        scratch_shapes=[pltpu.VMEM((count, width), BF16), pltpu.VMEM((total, TILE), BF16), pltpu.SemaphoreType.DMA((4,)),
                        pltpu.SemaphoreType.DMA((count // TILE,)), pltpu.SemaphoreType.DMA(())],
        compiler_params=pltpu.CompilerParams(vmem_limit_bytes=49 << 20),
        name="first_product",
    )(rows, weight)


def second_product_kernel(rows_ref, w_ref, *refs):
    outs, total_ref = refs[:4], refs[4]

    def body(tile, carry):
        span = pl.ds(pl.multiple_of(tile * TILE, TILE), TILE)
        total_ref[...] = lax.dot_general(
            rows_ref[...], w_ref[span, :], CONTRACT, preferred_element_type=F32).astype(BF16)
        scatter_rows(total_ref, outs, tile * TILE)
        return carry

    lax.fori_loop(0, outs[0].shape[1] // TILE, body, 0)


def second_product(rows, weight):
    total, count = rows.shape[0], weight.shape[0]
    return pl.pallas_call(
        second_product_kernel,
        out_shape=[pltpu.VMEM((total // 4, count), BF16)] * 4,
        in_specs=[VMEM_SPEC] * 2,
        out_specs=[VMEM_SPEC] * 4,
        scratch_shapes=[pltpu.VMEM((total, TILE), BF16)],
        compiler_params=SMALL,
        name="second_product",
    )(rows, weight)


def small(kernel, operands, shape, spec=None):
    return pl.pallas_call(
        kernel,
        out_shape=pltpu.VMEM(shape, BF16),
        in_specs=[spec or VMEM_SPEC] * len(operands),
        out_specs=VMEM_SPEC,
        scratch_shapes=[pltpu.SemaphoreType.DMA(())] if spec else [],
        compiler_params=pltpu.CompilerParams(vmem_limit_bytes=60 << 20) if spec else SMALL,
    )(*operands)


def quarter_kernel(rows_ref, out_ref, sem):
    hid = lax.axis_index("hid")
    tokens, half = out_ref.shape
    quarter = ((hid >> 2) & 1) * 2 + (hid & 1)
    source = rows_ref.at[pl.ds(pl.multiple_of(quarter * tokens, tokens), tokens),
                         pl.ds(pl.multiple_of((1 - lax.axis_index("rep")) * half, half), half)]
    copy = pltpu.make_async_copy(source, out_ref, sem)
    copy.start()
    copy.wait()


def join_kernel(a_ref, b_ref, out_ref):
    out_ref[...] = (a_ref[...].astype(F32) + b_ref[...].astype(F32)).astype(BF16)


def stack_kernel(a_ref, b_ref, out_ref):
    out_ref[0] = a_ref[...]
    out_ref[1] = b_ref[...]


def choose_kernel(a_ref, b_ref, out_ref):
    core = lax.axis_index("wid") & 1
    for number, source in enumerate((a_ref, b_ref)):
        @pl.when(core == number)
        def _():
            out_ref[...] = source[...]


def rotate_kernel(keep_ref, away_ref, far_ref, codes_ref, *refs, scale, start):
    outs, mixed_ref = refs[:-1], refs[-1]
    rows = outs[0].shape[0]
    mine = place(0)
    row = lax.broadcasted_iota(jnp.int32, (TILE, TILE), 0)
    col = lax.broadcasted_iota(jnp.int32, (TILE, TILE), 1)
    bits = row & col & (BLOCK - 1)
    for shift in (4, 2, 1):
        bits = bits ^ (bits >> shift)
    sign = (1 - 2 * (bits & 1)).astype(F32)
    table = jnp.where((row ^ col) < BLOCK, sign, 0.0).astype(BF16)
    for first in range(0, far_ref.shape[1], TILE):
        cols = pl.ds(first, TILE)
        total = keep_ref[:, cols].astype(F32) + away_ref[:, cols].astype(F32) + far_ref[:, cols].astype(F32)
        codes = codes_ref[:, pl.ds(start + first, TILE)]
        masked = jnp.where((codes > -128) & (codes < 127), total, 0.0).astype(BF16)
        mixed = jnp.dot(masked, table, preferred_element_type=F32)
        mixed_ref[:, cols] = (mixed * scale).astype(BF16)
    for step, out in enumerate(outs):
        out[...] = mixed_ref[pl.ds(pl.multiple_of((mine ^ step) * rows, rows), rows), :]


def rotate(sums, codes, start, scale):
    tokens, count = sums[0].shape
    return pl.pallas_call(
        functools.partial(rotate_kernel, scale=scale, start=start),
        out_shape=[pltpu.VMEM((tokens // 4, count), BF16)] * 4,
        in_specs=[VMEM_SPEC] * 4,
        out_specs=[VMEM_SPEC] * 4,
        scratch_shapes=[pltpu.VMEM((tokens, count), BF16)],
        compiler_params=SMALL,
        name="rotate",
    )(*sums, codes)


def parity(value):
    return (1 - 2 * ((value ^ (value >> 1)) & 1)).astype(F32)


def mix_kernel(*refs, axis):
    groups, outs = [refs[i:i + 4] for i in range(0, len(refs) - 4, 4)], refs[-4:]
    mine = place(axis)
    signs = [parity(mine & step) for step in range(4)]
    whole = parity(mine)
    start = 0
    for group in groups:
        for first in range(0, group[0].shape[1], TILE):
            here, cols = pl.ds(first, TILE), pl.ds(start + first, TILE)
            p0, p1, p2, p3 = [group[step][:, here].astype(F32) * signs[step] for step in range(4)]
            even, odd = (p0 + p1, p2 + p3), (p0 - p1, p2 - p3)
            mixed = (even[0] + even[1], odd[0] + odd[1], even[0] - even[1], odd[0] - odd[1])
            for step in range(4):
                outs[step][:, cols] = (mixed[step] * (whole * signs[step])).astype(BF16)
        start += group[0].shape[1]


def relabel_kernel(*refs):
    turn = place(0) ^ place(1)
    for step in range(4):
        for other in range(4):
            @pl.when(turn == step ^ other)
            def _():
                refs[4 + step][...] = refs[other][...]


def four(kernel, pieces):
    rows = pieces[0].shape[0]
    width = sum(piece.shape[1] for piece in pieces[::4])
    return pl.pallas_call(
        kernel,
        out_shape=[pltpu.VMEM((rows, width), BF16)] * 4,
        in_specs=[VMEM_SPEC] * len(pieces),
        out_specs=[VMEM_SPEC] * 4,
        compiler_params=SMALL,
    )(*pieces)


def finish_kernel(p0, p1, p2, p3, gate_ref, up_ref, gate_out, up_out, gate_buf, up_buf, sem):
    mine = place(1)
    rows = p0.shape[0]
    copies = []
    for step, piece in enumerate((p0, p1, p2, p3)):
        span = pl.ds(pl.multiple_of((mine ^ step) * rows, rows), rows)
        for first in range(0, piece.shape[1], TILE):
            cols = pl.ds(first, TILE)
            hidden = piece[:, cols].astype(F32)
            gate = gate_ref[span, cols].astype(F32)
            up = up_ref[span, cols].astype(F32)
            sig = jax.nn.sigmoid(gate)
            gate_buf[step, :, cols] = (hidden * up * sig * (1.0 + gate * (1.0 - sig))).astype(BF16)
            up_buf[step, :, cols] = (hidden * gate * sig).astype(BF16)
        copies.append(pltpu.make_async_copy(gate_buf.at[step], gate_out.at[span], sem.at[2 * step]))
        copies.append(pltpu.make_async_copy(up_buf.at[step], up_out.at[span], sem.at[2 * step + 1]))
        copies[-2].start()
        copies[-1].start()
    for copy in copies:
        copy.wait()


def finish(pieces, gate, up):
    shape = (4, *pieces[0].shape)
    return pl.pallas_call(
        finish_kernel,
        out_shape=[jax.ShapeDtypeStruct(gate.shape, BF16)] * 2,
        in_specs=[VMEM_SPEC] * 6,
        out_specs=[ANY_SPEC] * 2,
        scratch_shapes=[pltpu.VMEM(shape, BF16), pltpu.VMEM(shape, BF16), pltpu.SemaphoreType.DMA((8,))],
        compiler_params=SMALL,
        name="finish",
    )(*pieces, gate, up)


def arrange_kernel(g0, g1, g23, out_ref):
    hid = lax.axis_index("hid")
    core = lax.axis_index("wid") & 1
    quarter = ((hid >> 2) & 1) * 2 + (hid & 1)
    tokens = g0.shape[0]
    for source, flip in ((g0, 0), (g1, 1 + core), (g23.at[0], 2 - core), (g23.at[1], 3)):
        out_ref[pl.ds(pl.multiple_of((quarter ^ flip) * tokens, tokens), tokens), :] = source[...]


def arrange(g0, g1, g23):
    return pl.pallas_call(
        arrange_kernel,
        out_shape=pltpu.VMEM((4 * g0.shape[0], g0.shape[1]), BF16),
        in_specs=[VMEM_SPEC] * 3,
        out_specs=VMEM_SPEC,
        compiler_params=SMALL,
        name="arrange",
    )(g0, g1, g23)


def down_kernel(*refs, flips, summed, last, mine):
    count = len(flips)
    pieces, rows_ref = refs[:count], refs[count]
    acc_ref = refs[count + 1] if summed else None
    out_ref = refs[count + 1 + summed]
    wid = lax.axis_index("wid")
    tokens = pieces[0].shape[1]
    width = out_ref.shape[1]
    offset = lax.axis_index("rep") * width if mine else 0
    copies = []
    for number, first in enumerate(range(0, width, TILE)):
        cols = pl.ds(first, TILE)
        total = None
        for piece, flip in zip(pieces, flips):
            right = rows_ref[pl.ds(pl.multiple_of((wid ^ flip) * tokens, tokens), tokens),
                             pl.ds(pl.multiple_of(offset + first, TILE), TILE)]
            part = jnp.dot(piece[...], right, preferred_element_type=F32)
            total = part if total is None else total + part
        if summed:
            total = total + acc_ref[:, cols].astype(F32)
        if not last:
            out_ref[:, cols] = total.astype(BF16)
            continue
        buffer_ref, sem = refs[-2:]
        buffer_ref[number] = total
        copies.append(pltpu.make_async_copy(buffer_ref.at[number], out_ref.at[:, cols], sem.at[number]))
        copies[-1].start()
    for copy in copies:
        copy.wait()


def down(pieces, flips, rows, width, acc=None, last=False):
    hidden, _ = pieces[0].shape
    operands = (*pieces, rows) if acc is None else (*pieces, rows, acc)
    scratch = [pltpu.VMEM((width // TILE, hidden, TILE), F32), pltpu.SemaphoreType.DMA((width // TILE,))]
    return pl.pallas_call(
        functools.partial(
            down_kernel, flips=flips, summed=acc is not None, last=last, mine=rows.shape[1] > width),
        out_shape=jax.ShapeDtypeStruct((hidden, width), F32) if last else pltpu.VMEM((hidden, width), BF16),
        in_specs=[VMEM_SPEC] * len(operands),
        out_specs=ANY_SPEC if last else VMEM_SPEC,
        scratch_shapes=scratch if last else [],
        compiler_params=pltpu.CompilerParams(vmem_limit_bytes=24 << 20),
        name="down",
    )(*operands)


def shards(grad_out, down_weight, saved_gate, saved_up, saved_codes, exponents):
    rows = grad_out[0]
    codes = saved_codes[0]
    tokens = codes.shape[0]
    half = rows.shape[1] // 2
    scale = 1.0 / math.sqrt(BLOCK * 16)

    g0 = small(quarter_kernel, (rows,), (tokens, half), pl.BlockSpec(memory_space=pltpu.HBM))
    g0 = send(g0, to_rep)
    g1 = send(g0, lambda h, w, r: (h ^ (3 if w & 1 == 0 else 12), w, r))
    g23 = small(stack_kernel, (g0, g1), (2, tokens, half))
    g23 = send(g23, lambda h, w, r: (h ^ (12 if w & 1 == 0 else 3), w, r))

    own = dequant_t(codes, jnp.transpose(exponents, (2, 0, 1)))
    own_mate = send(own, to_mate)
    next_ = send(own, to_next)
    next_mate = send(next_, to_mate)

    sums = []
    for part, (first, count) in enumerate(PARTS):
        if part == 0:
            far_away, far_keep, near_away, near_keep, rows_near, rest = first_product(rows, down_weight, count)
        else:
            far_away, far_keep, near_away, near_keep = second_product(rows_near, rest)
        far_away = send(far_away, to_mate)
        near_away = send(near_away, to_mate)
        far = small(join_kernel, (far_keep, far_away), far_keep.shape)
        far = send(far, to_pair)
        sums.append((near_keep, near_away, far))

    pair = send(own, to_pair)
    pair_mate = send(pair, to_mate)
    cross = small(choose_kernel, (pair, next_), pair.shape)
    cross = send(cross, lambda h, w, r: (h, w ^ 2, r ^ 1 if w & 1 == 0 else r))
    cross_mate = send(cross, to_mate)

    product = down((own, own_mate), (0, 1), rows_near, half)
    other_rows = arrange(g0, g1, g23)
    product = down((next_, next_mate), (2, 3), other_rows, half, product)
    product = down((pair, pair_mate), (2, 3), rows_near, half, product)

    def spread(pieces, axis):
        moved = list(pieces)
        for step in (2, 1, 3):
            moved[step] = send(pieces[step], along(axis, step))
        return moved

    pieces = []
    for part, (first, count) in enumerate(PARTS):
        turned = rotate(sums[part], codes, first, scale)
        pieces += spread(turned, 0)
    pieces = four(functools.partial(mix_kernel, axis=0), pieces)
    pieces = spread(pieces, 0)
    pieces = four(relabel_kernel, pieces)
    pieces = spread(pieces, 1)
    pieces = four(functools.partial(mix_kernel, axis=1), pieces)
    pieces = spread(pieces, 1)
    grad_gate, grad_up = finish(pieces, saved_gate[0], saved_up[0])

    grad_down = down((cross, cross_mate), (0, 1), other_rows, half, product, last=True)
    return grad_gate[None], grad_up[None], grad_down


def solution(mesh):
    in_specs = (
        P("rep", None, "wid"),
        P("hid", "wid"),
        P("rep", "wid", "hid"),
        P("rep", "wid", "hid"),
        P("rep", "wid", "hid"),
        P("rep", "wid", "hid"),
    )
    out_specs = (P("rep", "wid", "hid"), P("rep", "wid", "hid"), P("hid", ("wid", "rep")))


    return jax.shard_map(shards, mesh=mesh, in_specs=in_specs, out_specs=out_specs, check_vma=False)
```
